1024 devices in a mesh: gx: 8 (over z_lo), gy: 16 (over y, core), gz: 8 (over x, z_hi).
Axes of the slice: x: 4, y: 8, z: 16 (z_hi: 2, z_lo: 8; z = z_hi * 8 + z_lo), core: 2. Of those that a mesh axis runs over, the one named last changes fastest.
Arguments:
- states: bfloat16 [192, 983040], P(None, ('gx', 'gy', 'gz')), may hold values from -16 to 16
- cell_matrices: bfloat16 [2048, 512, 512], P(('gx', 'gy', 'gz')), as said below
- connectivity: int32 [2048, 512], P(('gx', 'gy', 'gz')), may hold values from 0 to 959, as said below
- side_nodes: int32 [4, 122880], P(None, ('gx', 'gy', 'gz')), may hold values from 0 to 959, as said below
- top_nodes: int32 [2, 65536], P(None, ('gx', 'gy', 'gz')), may hold values from 0 to 959, as said below
- pot_index: int32 [983040], P(('gx', 'gy', 'gz')), may hold values from 0 to 63
- pot_table: float32 [64], replicated, may hold values from -1 to 1
Outputs:
- rotated: bfloat16 [192, 983040], P(None, ('gx', 'gy', 'gz'))
The draws below stay inside these ranges and needn't reach their ends.
Inputs may be any that keep to these rules, and one draw needn't show every extreme that they name: `connectivity`: slot numbers within one block; the nodes of one element take distinct slots. `side_nodes`: slot numbers within one block. `top_nodes`: slot numbers within one block. `cell_matrices`: each element's matrix is symmetric.
All inputs are finite; a program needn't handle non-finite values.
Results may differ from the reference program's by a relative error of at most 0.0067.
Values sent between devices are 32-bit elements; how exact they have to be, the bound alone decides.
A program may use at most 32 MiB of HBM per device.

```python
import math
import jax
import jax.numpy as jnp
import numpy as np
from jax import lax

STATES = 192
EDGE = 8
CELLS_DEV = 2
TABLE = 64
NODES_CELL = 512
LOCAL = 960
SIDE = 120
TOP = 64
NODES = 983040
CELLS = 2048
N_GX = 8
N_GY = 16
N_GZ = 8


def grid_slot(xpos, ypos, zpos):
    tall_nodes = 2 * EDGE - 1
    return (xpos * EDGE + ypos) * tall_nodes + zpos


def block_perms(key):
    blocks = CELLS // CELLS_DEV
    keys = jax.random.split(jax.random.fold_in(key, 7), blocks)
    return jax.vmap(lambda single: jax.random.permutation(single, LOCAL))(keys).astype(jnp.int32)


def cell_table():
    rows = []
    for elem_z in range(2):
        entries = []
        for along_a in range(EDGE):
            for along_b in range(EDGE):
                for along_c in range(EDGE):
                    entries.append(grid_slot(along_a, along_b, elem_z * (EDGE - 1) + along_c))
        rows.append(entries)
    return np.array(rows, dtype=np.int32)


def side_table():
    tall_nodes = 2 * EDGE - 1
    rows = []
    for level in (0, EDGE - 1):
        rows.append([grid_slot(level, ypos, zpos) for ypos in range(EDGE) for zpos in range(tall_nodes)])
    for level in (0, EDGE - 1):
        rows.append([grid_slot(xpos, level, zpos) for xpos in range(EDGE) for zpos in range(tall_nodes)])
    return np.array(rows, dtype=np.int32)


def top_table():
    tall_nodes = 2 * EDGE - 1
    rows = []
    for level in (0, tall_nodes - 1):
        rows.append([grid_slot(xpos, ypos, level) for xpos in range(EDGE) for ypos in range(EDGE)])
    return np.array(rows, dtype=np.int32)


def draw_connectivity(key, part):
    perms = block_perms(key)
    table = jnp.asarray(cell_table())
    picked = perms[:, table]
    return picked.reshape(CELLS, NODES_CELL).astype(jnp.int32)


def draw_side_nodes(key, part):
    perms = block_perms(key)
    table = jnp.asarray(side_table())
    picked = perms[:, table]
    return picked.transpose(1, 0, 2).reshape(4, -1).astype(jnp.int32)


def draw_top_nodes(key, part):
    perms = block_perms(key)
    table = jnp.asarray(top_table())
    picked = perms[:, table]
    return picked.transpose(1, 0, 2).reshape(2, -1).astype(jnp.int32)


def draw_cell_matrices(key, part):
    inner = jax.random.fold_in(key, 11)
    shape = (CELLS, NODES_CELL, NODES_CELL)
    raw = jax.random.normal(inner, shape, jnp.float32)
    sym = (raw + jnp.swapaxes(raw, 1, 2)) / jnp.sqrt(2.0)
    sym = jnp.clip(sym, -6.0, 6.0) / jnp.sqrt(float(NODES_CELL))
    return sym.astype(jnp.bfloat16)


def draw_states(key, part):
    keys = jax.random.split(jax.random.fold_in(key, 23), 5)
    shape = (STATES, NODES)
    shared_count = 4
    shared_weight = 0.35
    base = jnp.clip(jax.random.normal(keys[0], shape, jnp.float32), -4.0, 4.0)
    coeffs = shared_weight * jnp.clip(jax.random.normal(keys[1], (STATES, shared_count), jnp.float32), -3.0, 3.0)
    patterns = jnp.clip(jax.random.normal(keys[2], (shared_count, NODES), jnp.float32), -3.0, 3.0)
    shared = jnp.dot(coeffs, patterns, precision=lax.Precision.HIGHEST)
    column = jnp.exp(jax.random.uniform(keys[3], (1, NODES), jnp.float32, math.log(0.25), math.log(2.5)))
    row = jnp.exp(jax.random.uniform(keys[4], (STATES, 1), jnp.float32, math.log(0.7), math.log(1.4)))
    blocks = NODES // LOCAL
    place = (jnp.arange(NODES, dtype=jnp.int32) // LOCAL).astype(jnp.float32) / float(max(blocks - 1, 1))
    rise = jnp.exp(0.5 * math.log(3.0) * place)[None, :]
    values = row * column * rise * (base + shared)
    return jnp.clip(values, -16.0, 16.0).astype(jnp.bfloat16)


def with_ends(drawn, own_key, least, top_value):
    longest = drawn.shape.index(max(drawn.shape))
    spots = []
    for shift in (0, 1):
        where = [jax.random.randint(jax.random.fold_in(own_key, axis), (), 0, length) for axis, length in enumerate(drawn.shape)]
        where[longest] = (where[longest] + shift) % drawn.shape[longest]
        spots.append(tuple(where))
    return drawn.at[spots[0]].set(least).at[spots[1]].set(top_value)


def setup_inputs(seed: int = 0) -> dict:
    arg_keys = jax.random.split(jax.random.key(seed), 8)
    states = draw_states(jax.random.fold_in(arg_keys[7], 71), 0)
    cell_matrices = draw_cell_matrices(jax.random.fold_in(arg_keys[7], 71), 0)
    connectivity = draw_connectivity(jax.random.fold_in(arg_keys[7], 71), 0)
    side_nodes = draw_side_nodes(jax.random.fold_in(arg_keys[7], 71), 0)
    top_nodes = draw_top_nodes(jax.random.fold_in(arg_keys[7], 71), 0)
    pot_index = with_ends(jax.random.randint(arg_keys[5], (NODES,), 0, TABLE), jax.random.fold_in(arg_keys[5], 1), 0, TABLE - 1).astype(jnp.int32)
    pot_table = jnp.clip(jax.random.uniform(arg_keys[6], (TABLE,), jnp.float32, -1.0, 1.0), -1.0, 1.0)
    return {"states": states, "cell_matrices": cell_matrices, "connectivity": connectivity, "side_nodes": side_nodes, "top_nodes": top_nodes, "pot_index": pot_index, "pot_table": pot_table}


def cell_part(item):
    field, mats, conn = item
    cols = jnp.take(field, conn, axis=1).reshape(STATES, CELLS_DEV, NODES_CELL)
    prod = jnp.einsum('cij,scj->sci', mats.astype(jnp.float32), cols.astype(jnp.float32))
    zeros = jnp.zeros((STATES, LOCAL), jnp.float32)
    return zeros.at[:, conn].add(prod.reshape(STATES, CELLS_DEV * NODES_CELL))

def shift_axis(values, axis, upward):
    count = values.shape[axis]
    empty = jnp.zeros_like(lax.slice_in_dim(values, 0, 1, axis=axis))
    if upward:
        return jnp.concatenate([empty, lax.slice_in_dim(values, 0, count - 1, axis=axis)], axis=axis)
    return jnp.concatenate([lax.slice_in_dim(values, 1, count, axis=axis), empty], axis=axis)

def add_pair(block_sum, low_list, up_list, low_got, up_got):
    return block_sum.at[:, low_list].add(low_got).at[:, up_list].add(up_got)

def reference(states, cell_matrices, connectivity, side_nodes, top_nodes, pot_index, pot_table):
    blocks = N_GX * N_GY * N_GZ
    mats = cell_matrices.reshape(blocks, CELLS_DEV, NODES_CELL, NODES_CELL)
    conn = connectivity.reshape(blocks, CELLS_DEV * NODES_CELL).astype(jnp.int32)
    sides = side_nodes.reshape(4, blocks, SIDE).transpose(1, 0, 2).astype(jnp.int32)
    tops = top_nodes.reshape(2, blocks, TOP).transpose(1, 0, 2).astype(jnp.int32)
    face_lists = [(sides[:, 0], sides[:, 1]), (sides[:, 2], sides[:, 3]), (tops[:, 0], tops[:, 1])]
    potential = pot_table[pot_index.astype(jnp.int32)].reshape(blocks, 1, LOCAL)
    picker = jax.vmap(lambda values, index: values[:, index])

    def apply(field):
        rounded = field.astype(jnp.bfloat16)
        cellsum = lax.map(cell_part, (rounded, mats, conn))
        total = cellsum
        for direction in range(3):
            low_list, up_list = face_lists[direction]
            count = low_list.shape[1]
            low_vals = picker(cellsum, low_list).reshape(N_GX, N_GY, N_GZ, STATES, count)
            up_vals = picker(cellsum, up_list).reshape(N_GX, N_GY, N_GZ, STATES, count)
            low_got = shift_axis(up_vals, direction, True).reshape(blocks, STATES, count)
            up_got = shift_axis(low_vals, direction, False).reshape(blocks, STATES, count)
            total = jax.vmap(add_pair)(total, low_list, up_list, low_got, up_got)
        return total + potential * field
    start = states.astype(jnp.float32).reshape(STATES, blocks, LOCAL).transpose(1, 0, 2)
    first = (apply(start) - 0.5 * start) / 3.0
    second = 2.0 * (apply(first) - 0.5 * first) / 3.0 - start
    filtered = second.astype(jnp.bfloat16).transpose(1, 0, 2).reshape(STATES, NODES)
    correlation = jnp.dot(filtered.astype(jnp.float32), filtered.T.astype(jnp.float32), preferred_element_type=jnp.float32) / NODES
    lower = jnp.linalg.cholesky(correlation)
    inverse = jax.scipy.linalg.solve_triangular(lower, jnp.eye(STATES, dtype=jnp.float32), lower=True)
    inverse = inverse.astype(jnp.bfloat16)
    return jnp.dot(inverse.astype(jnp.float32), filtered.astype(jnp.float32), preferred_element_type=jnp.float32).astype(jnp.bfloat16)
```

```python
import functools
import jax
import jax.numpy as jnp
from jax import lax
from jax.experimental import pallas as pl
from jax.experimental.pallas import tpu as pltpu
from jax.sharding import PartitionSpec as P

MESH = pl.DeviceIdType.MESH
f32, bf16, i32 = jnp.float32, jnp.bfloat16, jnp.int32
WIDE = 1024
TILE = 512
HALF = 64


def half_tile(q):
    if q < 48:
        return 4 * q, 0
    return 128 + 4 * (q - 48), 128


def matmul(a, b, transposed=False):
    dims = (((1,), (1 if transposed else 0,)), ((), ()))
    return lax.dot_general(a, b, dims, preferred_element_type=f32)


def filter_kernel(
    sizes, table, conn, side, top, pidx, x_ref, k_ref, filt, gram,
    zeros, lists, inside, shift, xpad, rounded, cols, parts, cparts, pparts, zparts, csum, first, nodes, faces,
    snd_z, snd_p, rcv_z, rcv_p, part, got1, got2, got3, wide,
    hsend, hrecv, sends, recvs,
):
    ngx, ngy, ngz = sizes
    members, ring = ngy * (ngz // 2), 2 * ngx
    slots = x_ref.shape[1]
    corner = k_ref.shape[1]
    states = x_ref.shape[0]
    half = states // 2
    gx, gy, gz = lax.axis_index("gx"), lax.axis_index("gy"), lax.axis_index("gz")
    zhi, xq = lax.rem(gz, 2), gz // 2
    me = xq * ngy + gy
    zpos = zhi * ngx + gx
    here = {"gz": gz, "gx": gx, "gy": gy}

    def member(j):
        return {"gx": gx, "gy": lax.rem(j, ngy), "gz": (j // ngy) * 2 + zhi}

    def along_z(j):
        return {"gx": lax.rem(j, ngx), "gy": gy, "gz": xq * 2 + j // ngx}

    def step(axis, delta):
        return {**here, axis: here[axis] + delta}

    links = (("gz", -1, ngz), ("gz", 1, ngz), ("gx", -1, ngx), ("gx", 1, ngx), ("gy", -1, ngy), ("gy", 1, ngy))

    def exists(axis, delta, size):
        return here[axis] > 0 if delta < 0 else here[axis] < size - 1

    barrier = pltpu.get_barrier_semaphore()

    @pl.loop(1, members)
    def _(off):
        pl.semaphore_signal(barrier, inc=1, device_id=member(lax.rem(me + off, members)), device_id_type=MESH)

    @pl.loop(1, ring)
    def _(off):
        pl.semaphore_signal(barrier, inc=1, device_id=along_z(lax.rem(zpos + off, ring)), device_id_type=MESH)

    crosses = jnp.logical_or(jnp.logical_and(zhi == 1, gz < ngz - 1), jnp.logical_and(zhi == 0, gz > 0))

    @pl.when(crosses)
    def _():
        pl.semaphore_signal(barrier, inc=1, device_id=step("gz", 2 * zhi - 1), device_id_type=MESH)

    zeros[...] = jnp.zeros(zeros.shape, f32)
    lists[...] = jnp.full(lists.shape, -1, i32)
    lists[0:2, 0 : top.shape[1]] = top[...]
    lists[2:6, 0 : side.shape[1]] = side[...]
    plain = lists[...]
    rolled = pltpu.roll(plain, 64, 1)
    rows = [plain[0:1], plain[1:2], rolled[0:1], rolled[1:2], plain[2:3], plain[3:4], plain[4:5], plain[5:6]]
    chunk = 64

    @pl.loop(0, WIDE // chunk)
    def _(c):
        base = pl.multiple_of(c * chunk, chunk)
        level = lax.broadcasted_iota(i32, (chunk, 128), 0) + base
        for e in range(2):
            for b in range(corner // 128):
                col = e * corner + b * 128
                row = conn[e : e + 1, b * 128 : (b + 1) * 128]
                nodes[pl.ds(base, chunk), col : col + 128] = jnp.where(level == row, 1.0, 0.0).astype(bf16)
        for b, row in enumerate(rows):
            faces[pl.ds(base, chunk), b * 128 : (b + 1) * 128] = jnp.where(level == row, 1.0, 0.0).astype(bf16)

    inside[...] = jnp.full(inside.shape, -1, i32)
    inside[:, 0:slots] = pidx[...]
    index = inside[...]
    value = jnp.zeros((1, WIDE), f32)
    for t in range(table.shape[0]):
        value = jnp.where(index == t, table[t], value)
    shift[...] = value - 0.5
    xpad[:, WIDE - 128 : WIDE] = jnp.zeros((states, 128), bf16)
    xpad[:, 0:slots] = x_ref[...]

    def tiles(body):
        @pl.loop(0, WIDE // TILE)
        def _(n):
            body(pl.ds(pl.multiple_of(n * TILE, TILE), TILE))

    def put_split(ref, where, v):
        high = v.astype(bf16)
        ref[0 : v.shape[0], where] = high
        ref[v.shape[0] : 2 * v.shape[0], where] = (v - high.astype(f32)).astype(bf16)

    def joined(both):
        return both[: both.shape[0] // 2] + both[both.shape[0] // 2 :]

    def cell_sum(field):
        def gather(t):
            cols[:, t] = matmul(field[...], nodes[:, t]).astype(bf16)

        tiles(gather)

        @pl.loop(0, 2)
        def _(e):
            t = pl.ds(pl.multiple_of(e * corner, corner), corner)
            put_split(parts, t, matmul(cols[:, t], k_ref[e]))

        def scatter(t):
            v = joined(matmul(parts[...], nodes[t, :], True))
            csum[:, t] = v
            put_split(cparts, t, v)

        tiles(scatter)

    def exchange(a):
        zz = jnp.zeros((half, 256), f32)
        for h in range(2):
            for p in range(2):
                top_row = p * states + h * half
                zz = zz + matmul(cparts[top_row : top_row + half, :], faces[:, h * 256 : (h + 1) * 256])
        snd_z[a, 0] = zz[:, 0:128]
        snd_z[a, 1] = zz[:, 128:256]
        planes = joined(matmul(cparts[...], faces[:, 512:1024]))
        for d in range(4):
            snd_p[a, d] = planes[:, d * 128 : (d + 1) * 128]
        copies = []
        for d, link in enumerate(links):
            axis, delta, size = link
            src = snd_z.at[a, d] if d < 2 else snd_p.at[a, d - 2]
            dst = rcv_z.at[a, d ^ 1] if d < 2 else rcv_p.at[a, (d - 2) ^ 1]
            into = rcv_z.at[a, d] if d < 2 else rcv_p.at[a, d - 2]
            copy = pltpu.make_async_remote_copy(
                src_ref=src, dst_ref=dst, send_sem=hsend.at[a, d], recv_sem=hrecv.at[a, d ^ 1],
                device_id=step(axis, delta), device_id_type=MESH,
            )
            arrival = pltpu.make_async_remote_copy(
                src_ref=src, dst_ref=into, send_sem=hsend.at[a, d], recv_sem=hrecv.at[a, d],
                device_id=step(axis, delta), device_id_type=MESH,
            )
            there = exists(*link)

            @pl.when(there)
            def _():
                copy.start()

            @pl.when(jnp.logical_not(there))
            def _():
                empty = zeros.at[pl.ds(0, half)] if d < 2 else zeros
                pltpu.make_async_copy(empty, into, hrecv.at[a, d]).start()

            copies.append((there, copy, arrival))
        return copies

    def arrive(a, copies, finish):
        for _, _, arrival in copies:
            arrival.wait_recv()
        for d in range(4):
            put_split(pparts, slice(d * 128, (d + 1) * 128), rcv_p[a, d])
        for d in range(2):
            put_split(zparts, slice(d * 128, (d + 1) * 128), rcv_z[a, d])

        def add(t):
            planes = joined(matmul(pparts[...], faces[t, 512:1024], True))
            for h in range(2):
                zz = joined(matmul(zparts[...], faces[t, h * 256 : (h + 1) * 256], True))
                r = slice(h * half, (h + 1) * half)
                finish(r, t, csum[r, t] + planes[r] + zz)

        tiles(add)

    cell_sum(xpad)
    pl.semaphore_wait(barrier, members - 1 + ring - 1 + jnp.where(crosses, 1, 0))
    copies0 = exchange(0)

    def finish_first(r, t, total):
        v = (total + shift[:, t] * xpad[r, t].astype(f32)) / 3.0
        first[r, t] = v
        rounded[r, t] = v.astype(bf16)

    arrive(0, copies0, finish_first)
    cell_sum(rounded)
    copies1 = exchange(1)

    def finish_second(r, t, total):
        v = 2.0 * (total + shift[:, t] * first[r, t]) / 3.0 - xpad[r, t].astype(f32)
        rounded[r, t] = v.astype(bf16)

    arrive(1, copies1, finish_second)
    filt[...] = rounded[:, 0:slots]
    wide[:, 128:256] = jnp.zeros((states, 128), f32)
    wide[:, 0:states] = matmul(rounded[...], rounded[...], True)

    count = HALF // members
    for q in range(HALF):
        r, c = half_tile(q)
        part[q // count, q % count] = wide[r : r + 4, c : c + 128]
    got1[me] = part[me]

    @pl.loop(1, members)
    def _(off):
        j = lax.rem(me + off, members)
        pltpu.make_async_remote_copy(
            src_ref=part.at[j], dst_ref=got1.at[me], send_sem=sends.at[0], recv_sem=recvs.at[0],
            device_id=member(j), device_id_type=MESH,
        ).start()

    def all_of(ref, n, s):
        return pltpu.make_async_remote_copy(
            src_ref=ref.at[pl.ds(0, n)], dst_ref=ref.at[pl.ds(0, n)], send_sem=sends.at[s], recv_sem=recvs.at[s],
            device_id=along_z(lax.rem(zpos + 1, ring)), device_id_type=MESH,
        )

    all_of(got1, members - 1, 0).wait_recv()
    got2[zpos] = jnp.sum(got1[...], axis=0)

    @pl.loop(1, ring)
    def _(off):
        pltpu.make_async_remote_copy(
            src_ref=got2.at[zpos], dst_ref=got2.at[zpos], send_sem=sends.at[1], recv_sem=recvs.at[1],
            device_id=along_z(lax.rem(zpos + off, ring)), device_id_type=MESH,
        ).start()

    all_of(got2, ring - 1, 1).wait_recv()
    got3[me] = jnp.sum(got2[...], axis=0)

    @pl.loop(1, members)
    def _(off):
        pltpu.make_async_remote_copy(
            src_ref=got3.at[me], dst_ref=got3.at[me], send_sem=sends.at[2], recv_sem=recvs.at[2],
            device_id=member(lax.rem(me + off, members)), device_id_type=MESH,
        ).start()

    all_of(got3, members - 1, 2).wait_recv()
    gram[0:128, 128:256] = jnp.zeros((128, 128), f32)
    for q in range(HALF):
        r, c = half_tile(q)
        gram[r : r + 4, c : c + 128] = got3[q // count, q % count]
    for there, copy, _ in copies0 + copies1:

        @pl.when(there)
        def _():
            copy.wait_send()

    all_of(got1, members - 1, 0).wait_send()
    all_of(got2, ring - 1, 1).wait_send()
    all_of(got3, members - 1, 2).wait_send()


def filtered_gram(sizes, table, conn, side, top, pidx, x, k):
    ngx, ngy, ngz = sizes
    members, ring = ngy * (ngz // 2), 2 * ngx
    count = HALF // members
    states, slots = x.shape
    whole = pl.BlockSpec(memory_space=pltpu.VMEM)
    halves = (count, 4, 128)
    return pl.pallas_call(
        functools.partial(filter_kernel, sizes),
        out_shape=(jax.ShapeDtypeStruct(x.shape, bf16), jax.ShapeDtypeStruct((states, 256), f32)),
        in_specs=[pl.BlockSpec(memory_space=pltpu.SMEM)] + [whole] * 6,
        out_specs=(whole, whole),
        scratch_shapes=[
            pltpu.VMEM((states, 128), f32),
            pltpu.VMEM((8, 128), i32),
            pltpu.VMEM((1, WIDE), i32),
            pltpu.VMEM((1, WIDE), f32),
            pltpu.VMEM((states, WIDE), bf16),
            pltpu.VMEM((states, WIDE), bf16),
            pltpu.VMEM((states, WIDE), bf16),
            pltpu.VMEM((2 * states, WIDE), bf16),
            pltpu.VMEM((2 * states, WIDE), bf16),
            pltpu.VMEM((2 * states, 512), bf16),
            pltpu.VMEM((states, 256), bf16),
            pltpu.VMEM((states, WIDE), f32),
            pltpu.VMEM((states, WIDE), f32),
            pltpu.VMEM((WIDE, 1024), bf16),
            pltpu.VMEM((WIDE, 1024), bf16),
            pltpu.VMEM((2, 2, states // 2, 128), f32),
            pltpu.VMEM((2, 4, states, 128), f32),
            pltpu.VMEM((2, 2, states // 2, 128), f32),
            pltpu.VMEM((2, 4, states, 128), f32),
            pltpu.VMEM((members, *halves), f32),
            pltpu.VMEM((members, *halves), f32),
            pltpu.VMEM((ring, *halves), f32),
            pltpu.VMEM((members, *halves), f32),
            pltpu.VMEM((states, 256), f32),
            pltpu.SemaphoreType.DMA((2, 6)),
            pltpu.SemaphoreType.DMA((2, 6)),
            pltpu.SemaphoreType.DMA((3,)),
            pltpu.SemaphoreType.DMA((3,)),
        ],
        compiler_params=pltpu.CompilerParams(collective_id=0, has_side_effects=True, vmem_limit_bytes=56 << 20),
        name="filter_gram",
    )(table, conn, side, top, pidx, x, k)


def eliminate(a_ref, states):
    groups = states // 8
    lane = lax.broadcasted_iota(i32, (1, 256), 1)
    sub = lax.broadcasted_iota(i32, (8, 1), 0)
    a = [a_ref[8 * g : 8 * g + 8, :] for g in range(groups)]
    for g in range(groups):
        for t in range(8):
            k = 8 * g + t
            row = a[g][t : t + 1, :]
            scaled = (row + jnp.where(lane == k, 1.0, 0.0)) * (1.0 / row[:, k : k + 1])
            for h in range(g + 1, groups):
                a[h] = a[h] - a[h][:, k : k + 1] * scaled
            a[g] = a[g] - jnp.where(sub > t, a[g][:, k : k + 1], 0.0) * scaled
        a_ref[8 * g : 8 * g + 8, :] = a[g]


def rotate_kernel(total_slots, gram, filt, out, work):
    states = filt.shape[0]
    work[...] = gram[...] * (1.0 / total_slots)
    work[0:128, 128:states] = work[128:states, 0:128].T
    full = work[...]
    row = lax.broadcasted_iota(i32, full.shape, 0)
    col = lax.broadcasted_iota(i32, full.shape, 1)
    diag = jnp.where(row == col, full, 0.0)
    across = jnp.sum(diag, axis=0, keepdims=True)
    across = lax.rsqrt(jnp.where(col[0:1] < states, across, 1.0))
    down = lax.rsqrt(jnp.sum(diag, axis=1, keepdims=True))
    work[...] = full * across * down
    eliminate(work, states)
    done = work[...]
    pivot = jnp.sum(jnp.where(row == col, done, 0.0), axis=1, keepdims=True)
    lower = jnp.where(col < row, done, jnp.where(col == row, 1.0, 0.0))
    inverse = (lower * lax.rsqrt(pivot) * across)[:, :states].astype(bf16)
    out[...] = matmul(inverse, filt[...]).astype(bf16)


def rotated(total_slots, gram, filt):
    whole = pl.BlockSpec(memory_space=pltpu.VMEM)
    return pl.pallas_call(
        functools.partial(rotate_kernel, total_slots),
        out_shape=jax.ShapeDtypeStruct(filt.shape, bf16),
        in_specs=[whole] * 2,
        out_specs=whole,
        scratch_shapes=[pltpu.VMEM(gram.shape, f32)],
        name="rotate",
    )(gram, filt)


def on_device(sizes, states, cell_matrices, connectivity, side_nodes, top_nodes, pot_index, pot_table):
    filt, gram = filtered_gram(
        sizes, pot_table, connectivity, side_nodes, top_nodes, pot_index[None, :], states, cell_matrices
    )
    total_slots = states.shape[1] * sizes[0] * sizes[1] * sizes[2]
    return rotated(total_slots, gram, filt)


def solution(mesh):
    sizes = tuple(mesh.shape[name] for name in ("gx", "gy", "gz"))
    in_specs = (
        P(None, ("gx", "gy", "gz")),
        P(("gx", "gy", "gz"), None, None),
        P(("gx", "gy", "gz"), None),
        P(None, ("gx", "gy", "gz")),
        P(None, ("gx", "gy", "gz")),
        P(("gx", "gy", "gz")),
        P(),
    )
    out_specs = P(None, ("gx", "gy", "gz"))
    return jax.shard_map(
        functools.partial(on_device, sizes), mesh=mesh, in_specs=in_specs, out_specs=out_specs, check_vma=False
    )
```

```python
import functools
import jax
import jax.numpy as jnp
from jax import lax
from jax.experimental import pallas as pl
from jax.experimental.pallas import tpu as pltpu
from jax.sharding import PartitionSpec as P

MESH = pl.DeviceIdType.MESH
f32, bf16, i32 = jnp.float32, jnp.bfloat16, jnp.int32
WIDE = 1024
TILE = 512
HALF = 64


def half_tile(q):
    if q < 48:
        return 4 * q, 0
    return 128 + 4 * (q - 48), 128


def matmul(a, b, transposed=False):
    dims = (((1,), (1 if transposed else 0,)), ((), ()))
    return lax.dot_general(a, b, dims, preferred_element_type=f32)


def filter_kernel(
    sizes, table, conn, side, top, pidx, x_ref, k_ref, filt, gram,
    zeros, lists, inside, shift, xpad, rounded, cols, parts, cparts, pparts, zparts, csum, first, nodes, faces, cellmat, facemat,
    snd_z, snd_p, rcv_z, rcv_p, part, got1, got2, got3, wide,
    hsend, hrecv, sends, recvs,
):
    ngx, ngy, ngz = sizes
    members, ring = ngy * (ngz // 2), 2 * ngx
    slots = x_ref.shape[1]
    corner = k_ref.shape[1]
    states = x_ref.shape[0]
    half = states // 2
    gx, gy, gz = lax.axis_index("gx"), lax.axis_index("gy"), lax.axis_index("gz")
    zhi, xq = lax.rem(gz, 2), gz // 2
    me = xq * ngy + gy
    zpos = zhi * ngx + gx
    here = {"gz": gz, "gx": gx, "gy": gy}

    def wrap(v, n):
        return jnp.where(v >= n, v - n, v)

    def far_first(i, n):
        even = lax.rem(i, 2) == 0
        return n // 2 + jnp.where(even, i // 2, -((i + 1) // 2))

    def over_plane(body):
        for ox in sorted(range(ngz // 2), key=lambda v: -min(v, ngz // 2 - v)):
            x = wrap(xq + ox, ngz // 2)

            @pl.loop(0, ngy if ox else ngy - 1)
            def _(i):
                y = wrap(gy + far_first(i, ngy), ngy)
                body(x * ngy + y, {"gx": gx, "gy": y, "gz": 2 * x + zhi})

    def over_ring(body):
        @pl.loop(0, ring - 1)
        def _(i):
            z = wrap(zpos + far_first(i, ring), ring)
            high = jnp.where(z >= ngx, 1, 0)
            body({"gx": z - high * ngx, "gy": gy, "gz": 2 * xq + high})

    def step(axis, delta):
        return {**here, axis: here[axis] + delta}

    links = (("gz", -1, ngz), ("gz", 1, ngz), ("gx", -1, ngx), ("gx", 1, ngx), ("gy", -1, ngy), ("gy", 1, ngy))

    def exists(axis, delta, size):
        return here[axis] > 0 if delta < 0 else here[axis] < size - 1

    barrier = pltpu.get_barrier_semaphore()

    def greet(place):
        pl.semaphore_signal(barrier, inc=1, device_id=place, device_id_type=MESH)

    crosses = jnp.logical_or(jnp.logical_and(zhi == 1, gz < ngz - 1), jnp.logical_and(zhi == 0, gz > 0))

    @pl.when(crosses)
    def _():
        greet(step("gz", 2 * zhi - 1))

    over_ring(greet)
    over_plane(lambda j, place: greet(place))

    zeros[...] = jnp.zeros(zeros.shape, f32)
    lists[...] = jnp.full(lists.shape, -1, i32)
    lists[0:2, 0 : top.shape[1]] = top[...]
    lists[2:6, 0 : side.shape[1]] = side[...]
    plain = lists[...]
    rolled = pltpu.roll(plain, 64, 1)
    rows = [plain[0:1], plain[1:2], rolled[0:1], rolled[1:2], plain[2:3], plain[3:4], plain[4:5], plain[5:6]]
    chunk = 64

    @pl.loop(0, WIDE // chunk)
    def _(c):
        base = pl.multiple_of(c * chunk, chunk)
        level = lax.broadcasted_iota(i32, (chunk, 128), 0) + base
        for e in range(2):
            for b in range(corner // 128):
                col = e * corner + b * 128
                row = conn[e : e + 1, b * 128 : (b + 1) * 128]
                nodes[pl.ds(base, chunk), col : col + 128] = jnp.where(level == row, 1.0, 0.0).astype(bf16)
        for b, row in enumerate(rows):
            faces[pl.ds(base, chunk), b * 128 : (b + 1) * 128] = jnp.where(level == row, 1.0, 0.0).astype(bf16)

    inside[...] = jnp.full(inside.shape, -1, i32)
    inside[:, 0:slots] = pidx[...]
    index = inside[...]
    value = jnp.zeros((1, WIDE), f32)
    for t in range(table.shape[0]):
        value = jnp.where(index == t, table[t], value)
    shift[...] = value - 0.5
    xpad[:, WIDE - 128 : WIDE] = jnp.zeros((states, 128), bf16)
    xpad[:, 0:slots] = x_ref[...]

    def tiles(body):
        @pl.loop(0, WIDE // TILE)
        def _(n):
            body(pl.ds(pl.multiple_of(n * TILE, TILE), TILE))

    def put_split(ref, where, v):
        high = v.astype(bf16)
        ref[0 : v.shape[0], where] = high
        ref[v.shape[0] : 2 * v.shape[0], where] = (v - high.astype(f32)).astype(bf16)

    def joined(both):
        return both[: both.shape[0] // 2] + both[both.shape[0] // 2 :]

    def cell_sum(field):
        def gather(t):
            cols[:, t] = matmul(field[...], nodes[:, t]).astype(bf16)

        tiles(gather)

        @pl.loop(0, 2)
        def _(e):
            t = pl.ds(pl.multiple_of(e * corner, corner), corner)
            put_split(parts, t, matmul(cols[:, t], k_ref[e]))

        def scatter(t):
            v = joined(matmul(parts[...], nodes[t, :], True))
            csum[:, t] = v
            put_split(cparts, t, v)

        tiles(scatter)

    def landing(a, d):
        return rcv_z.at[a, d] if d < 2 else rcv_p.at[a, d - 2]

    def outgoing(a, d):
        axis, delta, size = links[d]
        return pltpu.make_async_remote_copy(
            src_ref=snd_z.at[a, d] if d < 2 else snd_p.at[a, d - 2], dst_ref=landing(a, d ^ 1),
            send_sem=hsend.at[a, d], recv_sem=hrecv.at[a, d ^ 1],
            device_id=step(axis, delta), device_id_type=MESH,
        )

    def incoming(a, d):
        axis, delta, size = links[d]
        return pltpu.make_async_remote_copy(
            src_ref=landing(a, d), dst_ref=landing(a, d), send_sem=hsend.at[a, d], recv_sem=hrecv.at[a, d],
            device_id=step(axis, delta), device_id_type=MESH,
        )

    def send(a, which):
        for d in which:
            there = exists(*links[d])

            @pl.when(there)
            def _():
                outgoing(a, d).start()

            @pl.when(jnp.logical_not(there))
            def _():
                empty = zeros.at[pl.ds(0, half)] if d < 2 else zeros
                pltpu.make_async_copy(empty, landing(a, d), hrecv.at[a, d]).start()

    def store_z(a, zz):
        snd_z[a, 0] = zz[:, 0:128]
        snd_z[a, 1] = zz[:, 128:256]

    def store_planes(a, planes):
        for d in range(4):
            snd_p[a, d] = planes[:, d * 128 : (d + 1) * 128]

    def arrive(a, finish):
        for d in range(2, 6):
            incoming(a, d).wait_recv()
        for d in range(4):
            put_split(pparts, slice(d * 128, (d + 1) * 128), rcv_p[a, d])

        def add_planes(t):
            csum[:, t] = csum[:, t] + joined(matmul(pparts[...], faces[t, 512:1024], True))

        tiles(add_planes)
        for d in range(2):
            incoming(a, d).wait_recv()
        for d in range(2):
            put_split(zparts, slice(d * 128, (d + 1) * 128), rcv_z[a, d])

        def add_z(t):
            for h in range(2):
                zz = joined(matmul(zparts[...], faces[t, h * 256 : (h + 1) * 256], True))
                r = slice(h * half, (h + 1) * half)
                finish(r, t, csum[r, t] + zz)

        tiles(add_z)

    cell_sum(xpad)
    zz = jnp.zeros((half, 256), f32)
    for h in range(2):
        for p in range(2):
            top_row = p * states + h * half
            zz = zz + matmul(cparts[top_row : top_row + half, :], faces[:, h * 256 : (h + 1) * 256])
    store_z(0, zz)
    store_planes(0, joined(matmul(cparts[...], faces[:, 512:1024])))
    pl.semaphore_wait(barrier, members - 1 + ring - 1 + jnp.where(crosses, 1, 0))
    send(0, range(6))

    @pl.loop(0, 2)
    def _(e):
        c = pl.ds(pl.multiple_of(e * corner, corner), corner)

        def spread_cell(t):
            cellmat[c, t] = matmul(k_ref[e], nodes[t, c], True).astype(bf16)

        tiles(spread_cell)

        def spread_faces(t):
            facemat[c, t] = matmul(cellmat[c, :], faces[:, t]).astype(bf16)

        tiles(spread_faces)

    def finish_first(r, t, total):
        v = (total + shift[:, t] * xpad[r, t].astype(f32)) / 3.0
        first[r, t] = v
        rounded[r, t] = v.astype(bf16)

    arrive(0, finish_first)

    def gather_second(t):
        cols[:, t] = matmul(rounded[...], nodes[:, t]).astype(bf16)

    tiles(gather_second)
    store_z(1, matmul(cols[0:half, :], facemat[:, 0:256]) + matmul(cols[half:states, :], facemat[:, 256:512]))
    send(1, range(2))
    store_planes(1, matmul(cols[...], facemat[:, 512:1024]))
    send(1, range(2, 6))

    def second_sum(t):
        csum[:, t] = matmul(cols[...], cellmat[:, t])

    tiles(second_sum)

    def finish_second(r, t, total):
        v = 2.0 * (total + shift[:, t] * first[r, t]) / 3.0 - xpad[r, t].astype(f32)
        rounded[r, t] = v.astype(bf16)

    wide[:, 128:256] = jnp.zeros((states, 128), f32)
    arrive(1, finish_second)
    wide[:, 0:states] = matmul(rounded[...], rounded[...], True)

    count = HALF // members
    for q in range(HALF):
        r, c = half_tile(q)
        part[q // count, q % count] = wide[r : r + 4, c : c + 128]
    got1[me] = part[me]

    def scatter(j, place):
        pltpu.make_async_remote_copy(
            src_ref=part.at[j], dst_ref=got1.at[me], send_sem=sends.at[0], recv_sem=recvs.at[0],
            device_id=place, device_id_type=MESH,
        ).start()

    over_plane(scatter)
    filt[...] = rounded[:, 0:slots]
    gram[0:128, 128:256] = jnp.zeros((128, 128), f32)

    def all_of(ref, n, s):
        return pltpu.make_async_remote_copy(
            src_ref=ref.at[pl.ds(0, n)], dst_ref=ref.at[pl.ds(0, n)], send_sem=sends.at[s], recv_sem=recvs.at[s],
            device_id={**here, "gy": wrap(gy + 1, ngy)}, device_id_type=MESH,
        )

    all_of(got1, members - 1, 0).wait_recv()
    got2[zpos] = jnp.sum(got1[...], axis=0)

    def along(place):
        pltpu.make_async_remote_copy(
            src_ref=got2.at[zpos], dst_ref=got2.at[zpos], send_sem=sends.at[1], recv_sem=recvs.at[1],
            device_id=place, device_id_type=MESH,
        ).start()

    over_ring(along)
    all_of(got2, ring - 1, 1).wait_recv()
    got3[me] = jnp.sum(got2[...], axis=0)

    def gather_all(j, place):
        pltpu.make_async_remote_copy(
            src_ref=got3.at[me], dst_ref=got3.at[me], send_sem=sends.at[2], recv_sem=recvs.at[2],
            device_id=place, device_id_type=MESH,
        ).start()

    over_plane(gather_all)
    all_of(got3, members - 1, 2).wait_recv()
    for q in range(HALF):
        r, c = half_tile(q)
        gram[r : r + 4, c : c + 128] = got3[q // count, q % count]
    for a in range(2):
        for d in range(6):

            @pl.when(exists(*links[d]))
            def _():
                outgoing(a, d).wait_send()

    all_of(got1, members - 1, 0).wait_send()
    all_of(got2, ring - 1, 1).wait_send()
    all_of(got3, members - 1, 2).wait_send()


def filtered_gram(sizes, table, conn, side, top, pidx, x, k):
    ngx, ngy, ngz = sizes
    members, ring = ngy * (ngz // 2), 2 * ngx
    count = HALF // members
    states, slots = x.shape
    whole = pl.BlockSpec(memory_space=pltpu.VMEM)
    halves = (count, 4, 128)
    return pl.pallas_call(
        functools.partial(filter_kernel, sizes),
        out_shape=(jax.ShapeDtypeStruct(x.shape, bf16), jax.ShapeDtypeStruct((states, 256), f32)),
        in_specs=[pl.BlockSpec(memory_space=pltpu.SMEM)] + [whole] * 6,
        out_specs=(whole, whole),
        scratch_shapes=[
            pltpu.VMEM((states, 128), f32),
            pltpu.VMEM((8, 128), i32),
            pltpu.VMEM((1, WIDE), i32),
            pltpu.VMEM((1, WIDE), f32),
            pltpu.VMEM((states, WIDE), bf16),
            pltpu.VMEM((states, WIDE), bf16),
            pltpu.VMEM((states, WIDE), bf16),
            pltpu.VMEM((2 * states, WIDE), bf16),
            pltpu.VMEM((2 * states, WIDE), bf16),
            pltpu.VMEM((2 * states, 512), bf16),
            pltpu.VMEM((states, 256), bf16),
            pltpu.VMEM((states, WIDE), f32),
            pltpu.VMEM((states, WIDE), f32),
            pltpu.VMEM((WIDE, 1024), bf16),
            pltpu.VMEM((WIDE, 1024), bf16),
            pltpu.VMEM((WIDE, 1024), bf16),
            pltpu.VMEM((WIDE, 1024), bf16),
            pltpu.VMEM((2, 2, states // 2, 128), f32),
            pltpu.VMEM((2, 4, states, 128), f32),
            pltpu.VMEM((2, 2, states // 2, 128), f32),
            pltpu.VMEM((2, 4, states, 128), f32),
            pltpu.VMEM((members, *halves), f32),
            pltpu.VMEM((members, *halves), f32),
            pltpu.VMEM((ring, *halves), f32),
            pltpu.VMEM((members, *halves), f32),
            pltpu.VMEM((states, 256), f32),
            pltpu.SemaphoreType.DMA((2, 6)),
            pltpu.SemaphoreType.DMA((2, 6)),
            pltpu.SemaphoreType.DMA((3,)),
            pltpu.SemaphoreType.DMA((3,)),
        ],
        compiler_params=pltpu.CompilerParams(collective_id=0, has_side_effects=True, vmem_limit_bytes=56 << 20),
        name="filter_gram",
    )(table, conn, side, top, pidx, x, k)


def eliminate(a_ref, states):
    groups = states // 8
    lane = lax.broadcasted_iota(i32, (8, 256), 1)
    sub = lax.broadcasted_iota(i32, (8, 256), 0)
    sub1 = sub[:, 0:128]

    def spread(v, k):
        return jnp.broadcast_to(v[:, k : k + 1], (8, 128))

    def twice(v):
        return jnp.concatenate([v, v], axis=1)

    def pivots(g, r):
        first = 8 * g
        c = [spread(r, first + t) for t in range(8)]
        keep = r
        scale = jnp.zeros((8, 128), f32)
        def full(v):
            return jnp.broadcast_to(v, (8, 128))

        for t in range(0, 8, 2):
            p, q, s = full(c[t][t : t + 1]), full(c[t + 1][t : t + 1]), full(c[t + 1][t + 1 : t + 2])
            one = 1.0 / p
            two = p * (1.0 / (p * s - q * q))
            m = jnp.where(sub1 == t, 0.0, c[t] * one)
            n = jnp.where(sub1 == t + 1, 0.0, (c[t + 1] - m * q) * two)
            for u in range(t + 2, 8):
                v = c[u] - m * c[u][t : t + 1]
                c[u] = v - n * v[t + 1 : t + 2]
            for k, inv, mult in ((t, one, m), (t + 1, two, n)):
                row = r[k : k + 1]
                keep = jnp.where(sub == k, row, keep)
                scale = jnp.where(sub1 == k, inv, scale)
                unit = jnp.where(lane[0:1] == first + k, 1.0, row)
                r = jnp.where(lane == first + k, jnp.where(sub == k, 1.0, 0.0), r) - twice(mult) * unit
        a_ref[first : first + 8, :] = keep
        return r * twice(scale)

    def update(g, r, v):
        first = 8 * g
        inside = jnp.logical_and(lane >= first, lane < first + 8)
        terms = [twice(spread(v, first + t)) * r[t : t + 1] for t in range(8)]
        while len(terms) > 1:
            terms = [terms[i] + terms[i + 1] for i in range(0, len(terms), 2)]
        return jnp.where(inside, 0.0, v) - terms[0]

    r = pivots(0, a_ref[0:8, :])
    for g in range(groups - 1):
        nxt = slice(8 * g + 8, 8 * g + 16)
        ahead = pivots(g + 1, update(g, r, a_ref[nxt, :]))
        for h in range(g + 2, groups):
            rows = slice(8 * h, 8 * h + 8)
            a_ref[rows, :] = update(g, r, a_ref[rows, :])
        r = ahead


def rotate_kernel(total_slots, gram, filt, out, work):
    states = filt.shape[0]
    work[...] = gram[...] * (1.0 / total_slots)
    work[0:128, 128:states] = work[128:states, 0:128].T
    full = work[...]
    row = lax.broadcasted_iota(i32, full.shape, 0)
    col = lax.broadcasted_iota(i32, full.shape, 1)
    diag = jnp.where(row == col, full, 0.0)
    across = jnp.sum(diag, axis=0, keepdims=True)
    across = lax.rsqrt(jnp.where(col[0:1] < states, across, 1.0))
    down = lax.rsqrt(jnp.sum(diag, axis=1, keepdims=True))
    work[...] = full * across * down
    eliminate(work, states)
    done = work[...]
    pivot = jnp.sum(jnp.where(row == col, done, 0.0), axis=1, keepdims=True)
    lower = jnp.where(col < row, done, jnp.where(col == row, 1.0, 0.0))
    inverse = (lower * lax.rsqrt(pivot) * across)[:, :states].astype(bf16)
    out[...] = matmul(inverse, filt[...]).astype(bf16)


def rotated(total_slots, gram, filt):
    whole = pl.BlockSpec(memory_space=pltpu.VMEM)
    return pl.pallas_call(
        functools.partial(rotate_kernel, total_slots),
        out_shape=jax.ShapeDtypeStruct(filt.shape, bf16),
        in_specs=[whole] * 2,
        out_specs=whole,
        scratch_shapes=[pltpu.VMEM(gram.shape, f32)],
        name="rotate",
    )(gram, filt)


def on_device(sizes, states, cell_matrices, connectivity, side_nodes, top_nodes, pot_index, pot_table):
    filt, gram = filtered_gram(
        sizes, pot_table, connectivity, side_nodes, top_nodes, pot_index[None, :], states, cell_matrices
    )
    total_slots = states.shape[1] * sizes[0] * sizes[1] * sizes[2]
    return rotated(total_slots, gram, filt)


def solution(mesh):
    sizes = tuple(mesh.shape[name] for name in ("gx", "gy", "gz"))
    in_specs = (
        P(None, ("gx", "gy", "gz")),
        P(("gx", "gy", "gz"), None, None),
        P(("gx", "gy", "gz"), None),
        P(None, ("gx", "gy", "gz")),
        P(None, ("gx", "gy", "gz")),
        P(("gx", "gy", "gz")),
        P(),
    )
    out_specs = P(None, ("gx", "gy", "gz"))
    return jax.shard_map(
        functools.partial(on_device, sizes), mesh=mesh, in_specs=in_specs, out_specs=out_specs, check_vma=False
    )
```

```python
import functools
import jax
import jax.numpy as jnp
from jax import lax
from jax.experimental import pallas as pl
from jax.experimental.pallas import tpu as pltpu
from jax.sharding import PartitionSpec as P

MESH = pl.DeviceIdType.MESH
f32, bf16, i32 = jnp.float32, jnp.bfloat16, jnp.int32
WIDE = 1024
TILE = 512
HALF = 64


def half_tile(q):
    if q < 48:
        return 4 * q, 0
    return 128 + 4 * (q - 48), 128


def matmul(a, b, transposed=False):
    dims = (((1,), (1 if transposed else 0,)), ((), ()))
    return lax.dot_general(a, b, dims, preferred_element_type=f32)


def filter_kernel(
    sizes, table, conn, side, top, pidx, x_hbm, k_hbm, filt, gram,
    zeros, lists, inside, shift, xpad, rounded, cols, parts, cparts, pparts, zparts, csum, first, nodes, faces, cellmat, facemat,
    snd_z, snd_p, rcv_z, rcv_p, part, got1, got2, got3, wide,
    x_ref, k_ref, fbuf, hsend, hrecv, sends, recvs, loads,
):
    ngx, ngy, ngz = sizes
    load_x = pltpu.make_async_copy(x_hbm, x_ref, loads.at[0])
    load_k = pltpu.make_async_copy(k_hbm, k_ref, loads.at[1])
    store_f = pltpu.make_async_copy(fbuf, filt, loads.at[2])
    load_x.start()
    load_k.start()
    members, ring = ngy * (ngz // 2), 2 * ngx
    slots = x_ref.shape[1]
    corner = k_ref.shape[1]
    states = x_ref.shape[0]
    half = states // 2
    gx, gy, gz = lax.axis_index("gx"), lax.axis_index("gy"), lax.axis_index("gz")
    zhi, xq = lax.rem(gz, 2), gz // 2
    me = xq * ngy + gy
    zpos = zhi * ngx + gx
    here = {"gz": gz, "gx": gx, "gy": gy}

    def wrap(v, n):
        return jnp.where(v >= n, v - n, v)

    def far_first(i, n):
        even = lax.rem(i, 2) == 0
        return n // 2 + jnp.where(even, i // 2, -((i + 1) // 2))

    def over_plane(body):
        for ox in sorted(range(ngz // 2), key=lambda v: -min(v, ngz // 2 - v)):
            x = wrap(xq + ox, ngz // 2)

            @pl.loop(0, ngy if ox else ngy - 1)
            def _(i):
                y = wrap(gy + far_first(i, ngy), ngy)
                body(x * ngy + y, {"gx": gx, "gy": y, "gz": 2 * x + zhi})

    def over_ring(body):
        @pl.loop(0, ring - 1)
        def _(i):
            z = wrap(zpos + far_first(i, ring), ring)
            high = jnp.where(z >= ngx, 1, 0)
            body({"gx": z - high * ngx, "gy": gy, "gz": 2 * xq + high})

    def step(axis, delta):
        return {**here, axis: here[axis] + delta}

    links = (("gz", -1, ngz), ("gz", 1, ngz), ("gx", -1, ngx), ("gx", 1, ngx), ("gy", -1, ngy), ("gy", 1, ngy))

    def exists(axis, delta, size):
        return here[axis] > 0 if delta < 0 else here[axis] < size - 1

    barrier = pltpu.get_barrier_semaphore()

    def greet(place):
        pl.semaphore_signal(barrier, inc=1, device_id=place, device_id_type=MESH)

    crosses = jnp.logical_or(jnp.logical_and(zhi == 1, gz < ngz - 1), jnp.logical_and(zhi == 0, gz > 0))

    @pl.when(crosses)
    def _():
        greet(step("gz", 2 * zhi - 1))

    over_ring(greet)
    over_plane(lambda j, place: greet(place))

    zeros[...] = jnp.zeros(zeros.shape, f32)
    lists[...] = jnp.full(lists.shape, -1, i32)
    lists[0:2, 0 : top.shape[1]] = top[...]
    lists[2:6, 0 : side.shape[1]] = side[...]
    plain = lists[...]
    rolled = pltpu.roll(plain, 64, 1)
    rows = [plain[0:1], plain[1:2], rolled[0:1], rolled[1:2], plain[2:3], plain[3:4], plain[4:5], plain[5:6]]
    chunk = 64

    @pl.loop(0, WIDE // chunk)
    def _(c):
        base = pl.multiple_of(c * chunk, chunk)
        level = lax.broadcasted_iota(i32, (chunk, 128), 0) + base
        for e in range(2):
            for b in range(corner // 128):
                col = e * corner + b * 128
                row = conn[e : e + 1, b * 128 : (b + 1) * 128]
                nodes[pl.ds(base, chunk), col : col + 128] = jnp.where(level == row, 1.0, 0.0).astype(bf16)
        for b, row in enumerate(rows):
            faces[pl.ds(base, chunk), b * 128 : (b + 1) * 128] = jnp.where(level == row, 1.0, 0.0).astype(bf16)

    inside[...] = jnp.full(inside.shape, -1, i32)
    inside[:, 0:slots] = pidx[...]
    index = inside[...]
    value = jnp.zeros((1, WIDE), f32)
    for t in range(table.shape[0]):
        value = jnp.where(index == t, table[t], value)
    shift[...] = value - 0.5
    xpad[:, WIDE - 128 : WIDE] = jnp.zeros((states, 128), bf16)
    load_x.wait()
    xpad[:, 0:slots] = x_ref[...]

    def tiles(body):
        @pl.loop(0, WIDE // TILE)
        def _(n):
            body(pl.ds(pl.multiple_of(n * TILE, TILE), TILE))

    def put_split(ref, where, v):
        high = v.astype(bf16)
        ref[0 : v.shape[0], where] = high
        ref[v.shape[0] : 2 * v.shape[0], where] = (v - high.astype(f32)).astype(bf16)

    def joined(both):
        return both[: both.shape[0] // 2] + both[both.shape[0] // 2 :]

    def first_sum(field):
        def gather(t):
            cols[:, t] = matmul(field[...], nodes[:, t]).astype(bf16)

        tiles(gather)
        load_k.wait()

        @pl.loop(0, 2)
        def _(e):
            t = pl.ds(pl.multiple_of(e * corner, corner), corner)
            put_split(parts, t, matmul(cols[:, t], k_ref[e]))

        def scatter(t):
            v = joined(matmul(parts[...], nodes[t, :], True))
            csum[:, t] = v
            put_split(cparts, t, v)

        tiles(scatter)

    def landing(a, d):
        return rcv_z.at[a, d] if d < 2 else rcv_p.at[a, d - 2]

    def outgoing(a, d):
        axis, delta, size = links[d]
        return pltpu.make_async_remote_copy(
            src_ref=snd_z.at[a, d] if d < 2 else snd_p.at[a, d - 2], dst_ref=landing(a, d ^ 1),
            send_sem=hsend.at[a, d], recv_sem=hrecv.at[a, d ^ 1],
            device_id=step(axis, delta), device_id_type=MESH,
        )

    def incoming(a, d):
        axis, delta, size = links[d]
        return pltpu.make_async_remote_copy(
            src_ref=landing(a, d), dst_ref=landing(a, d), send_sem=hsend.at[a, d], recv_sem=hrecv.at[a, d],
            device_id=step(axis, delta), device_id_type=MESH,
        )

    def send(a, which):
        for d in which:
            there = exists(*links[d])

            @pl.when(there)
            def _():
                outgoing(a, d).start()

            @pl.when(jnp.logical_not(there))
            def _():
                empty = zeros.at[pl.ds(0, half)] if d < 2 else zeros
                pltpu.make_async_copy(empty, landing(a, d), hrecv.at[a, d]).start()

    def store_z(a, zz):
        snd_z[a, 0] = zz[:, 0:128]
        snd_z[a, 1] = zz[:, 128:256]

    def store_planes(a, planes):
        for d in range(4):
            snd_p[a, d] = planes[:, d * 128 : (d + 1) * 128]

    def arrive(a, finish):
        for d in range(2, 6):
            incoming(a, d).wait_recv()
        for d in range(4):
            put_split(pparts, slice(d * 128, (d + 1) * 128), rcv_p[a, d])

        def add_planes(t):
            csum[:, t] = csum[:, t] + joined(matmul(pparts[...], faces[t, 512:1024], True))

        tiles(add_planes)
        for d in range(2):
            incoming(a, d).wait_recv()
        for d in range(2):
            put_split(zparts, slice(d * 128, (d + 1) * 128), rcv_z[a, d])

        def add_z(t):
            for h in range(2):
                zz = joined(matmul(zparts[...], faces[t, h * 256 : (h + 1) * 256], True))
                r = slice(h * half, (h + 1) * half)
                finish(r, t, csum[r, t] + zz)

        tiles(add_z)

    first_sum(xpad)
    zz = jnp.zeros((half, 256), f32)
    for h in range(2):
        for p in range(2):
            top_row = p * states + h * half
            zz = zz + matmul(cparts[top_row : top_row + half, :], faces[:, h * 256 : (h + 1) * 256])
    store_z(0, zz)
    pl.semaphore_wait(barrier, members - 1 + ring - 1 + jnp.where(crosses, 1, 0))
    send(0, range(2))
    store_planes(0, joined(matmul(cparts[...], faces[:, 512:1024])))
    send(0, range(2, 6))

    @pl.loop(0, 2)
    def _(e):
        c = pl.ds(pl.multiple_of(e * corner, corner), corner)

        def spread_cell(t):
            cellmat[c, t] = matmul(k_ref[e], nodes[t, c], True).astype(bf16)

        tiles(spread_cell)

        def spread_faces(t):
            facemat[c, t] = matmul(cellmat[c, :], faces[:, t]).astype(bf16)

        tiles(spread_faces)

    def finish_first(r, t, total):
        v = (total + shift[:, t] * xpad[r, t].astype(f32)) / 3.0
        first[r, t] = v
        rounded[r, t] = v.astype(bf16)

    arrive(0, finish_first)

    def gather_second(t):
        cols[:, t] = matmul(rounded[...], nodes[:, t]).astype(bf16)

    tiles(gather_second)
    store_z(1, matmul(cols[0:half, :], facemat[:, 0:256]) + matmul(cols[half:states, :], facemat[:, 256:512]))
    send(1, range(2))
    store_planes(1, matmul(cols[...], facemat[:, 512:1024]))
    send(1, range(2, 6))

    def second_sum(t):
        csum[:, t] = matmul(cols[...], cellmat[:, t])

    tiles(second_sum)

    def finish_second(r, t, total):
        v = 2.0 * (total + shift[:, t] * first[r, t]) / 3.0 - xpad[r, t].astype(f32)
        rounded[r, t] = v.astype(bf16)

    wide[:, 128:256] = jnp.zeros((states, 128), f32)
    arrive(1, finish_second)
    wide[:, 0:states] = matmul(rounded[...], rounded[...], True)

    count = HALF // members
    for q in range(HALF):
        r, c = half_tile(q)
        part[q // count, q % count] = wide[r : r + 4, c : c + 128]
    got1[me] = part[me]

    def scatter(j, place):
        pltpu.make_async_remote_copy(
            src_ref=part.at[j], dst_ref=got1.at[me], send_sem=sends.at[0], recv_sem=recvs.at[0],
            device_id=place, device_id_type=MESH,
        ).start()

    over_plane(scatter)
    fbuf[...] = rounded[:, 0:slots]
    store_f.start()
    gram[0:128, 128:256] = jnp.zeros((128, 128), f32)

    def all_of(ref, n, s):
        return pltpu.make_async_remote_copy(
            src_ref=ref.at[pl.ds(0, n)], dst_ref=ref.at[pl.ds(0, n)], send_sem=sends.at[s], recv_sem=recvs.at[s],
            device_id={**here, "gy": wrap(gy + 1, ngy)}, device_id_type=MESH,
        )

    all_of(got1, members - 1, 0).wait_recv()
    got2[zpos] = jnp.sum(got1[...], axis=0)

    def along(place):
        pltpu.make_async_remote_copy(
            src_ref=got2.at[zpos], dst_ref=got2.at[zpos], send_sem=sends.at[1], recv_sem=recvs.at[1],
            device_id=place, device_id_type=MESH,
        ).start()

    over_ring(along)
    all_of(got2, ring - 1, 1).wait_recv()
    got3[me] = jnp.sum(got2[...], axis=0)

    def gather_all(j, place):
        pltpu.make_async_remote_copy(
            src_ref=got3.at[me], dst_ref=got3.at[me], send_sem=sends.at[2], recv_sem=recvs.at[2],
            device_id=place, device_id_type=MESH,
        ).start()

    over_plane(gather_all)
    all_of(got3, members - 1, 2).wait_recv()
    for q in range(HALF):
        r, c = half_tile(q)
        gram[r : r + 4, c : c + 128] = got3[q // count, q % count]
    for a in range(2):
        for d in range(6):

            @pl.when(exists(*links[d]))
            def _():
                outgoing(a, d).wait_send()

    store_f.wait()
    all_of(got1, members - 1, 0).wait_send()
    all_of(got2, ring - 1, 1).wait_send()
    all_of(got3, members - 1, 2).wait_send()


def filtered_gram(sizes, table, conn, side, top, pidx, x, k):
    ngx, ngy, ngz = sizes
    members, ring = ngy * (ngz // 2), 2 * ngx
    count = HALF // members
    states, slots = x.shape
    whole = pl.BlockSpec(memory_space=pltpu.VMEM)
    far = pl.BlockSpec(memory_space=pl.ANY)
    halves = (count, 4, 128)
    return pl.pallas_call(
        functools.partial(filter_kernel, sizes),
        out_shape=(jax.ShapeDtypeStruct(x.shape, bf16), jax.ShapeDtypeStruct((states, 256), f32)),
        in_specs=[pl.BlockSpec(memory_space=pltpu.SMEM)] + [whole] * 4 + [far] * 2,
        out_specs=(far, whole),
        scratch_shapes=[
            pltpu.VMEM((states, 128), f32),
            pltpu.VMEM((8, 128), i32),
            pltpu.VMEM((1, WIDE), i32),
            pltpu.VMEM((1, WIDE), f32),
            pltpu.VMEM((states, WIDE), bf16),
            pltpu.VMEM((states, WIDE), bf16),
            pltpu.VMEM((states, WIDE), bf16),
            pltpu.VMEM((2 * states, WIDE), bf16),
            pltpu.VMEM((2 * states, WIDE), bf16),
            pltpu.VMEM((2 * states, 512), bf16),
            pltpu.VMEM((states, 256), bf16),
            pltpu.VMEM((states, WIDE), f32),
            pltpu.VMEM((states, WIDE), f32),
            pltpu.VMEM((WIDE, 1024), bf16),
            pltpu.VMEM((WIDE, 1024), bf16),
            pltpu.VMEM((WIDE, 1024), bf16),
            pltpu.VMEM((WIDE, 1024), bf16),
            pltpu.VMEM((2, 2, states // 2, 128), f32),
            pltpu.VMEM((2, 4, states, 128), f32),
            pltpu.VMEM((2, 2, states // 2, 128), f32),
            pltpu.VMEM((2, 4, states, 128), f32),
            pltpu.VMEM((members, *halves), f32),
            pltpu.VMEM((members, *halves), f32),
            pltpu.VMEM((ring, *halves), f32),
            pltpu.VMEM((members, *halves), f32),
            pltpu.VMEM((states, 256), f32),
            pltpu.VMEM(x.shape, bf16),
            pltpu.VMEM(k.shape, bf16),
            pltpu.VMEM(x.shape, bf16),
            pltpu.SemaphoreType.DMA((2, 6)),
            pltpu.SemaphoreType.DMA((2, 6)),
            pltpu.SemaphoreType.DMA((3,)),
            pltpu.SemaphoreType.DMA((3,)),
            pltpu.SemaphoreType.DMA((3,)),
        ],
        compiler_params=pltpu.CompilerParams(collective_id=0, has_side_effects=True, vmem_limit_bytes=56 << 20),
        name="filter_gram",
    )(table, conn, side, top, pidx, x, k)


def eliminate(a_ref, states):
    groups = states // 8
    lane = lax.broadcasted_iota(i32, (8, 256), 1)
    sub = lax.broadcasted_iota(i32, (8, 256), 0)
    sub1 = sub[:, 0:128]

    def spread(v, k):
        return jnp.broadcast_to(v[:, k : k + 1], (8, 128))

    def twice(v):
        return jnp.concatenate([v, v], axis=1)

    def pivots(g, r):
        first = 8 * g
        c = [spread(r, first + t) for t in range(8)]
        keep = r
        scale = jnp.zeros((8, 128), f32)
        def full(v):
            return jnp.broadcast_to(v, (8, 128))

        for t in range(0, 8, 2):
            p, q, s = full(c[t][t : t + 1]), full(c[t + 1][t : t + 1]), full(c[t + 1][t + 1 : t + 2])
            one = 1.0 / p
            two = p * (1.0 / (p * s - q * q))
            m = jnp.where(sub1 == t, 0.0, c[t] * one)
            n = jnp.where(sub1 == t + 1, 0.0, (c[t + 1] - m * q) * two)
            for u in range(t + 2, 8):
                v = c[u] - m * c[u][t : t + 1]
                c[u] = v - n * v[t + 1 : t + 2]
            for k, inv, mult in ((t, one, m), (t + 1, two, n)):
                row = r[k : k + 1]
                keep = jnp.where(sub == k, row, keep)
                scale = jnp.where(sub1 == k, inv, scale)
                unit = jnp.where(lane[0:1] == first + k, 1.0, row)
                r = jnp.where(lane == first + k, jnp.where(sub == k, 1.0, 0.0), r) - twice(mult) * unit
        a_ref[first : first + 8, :] = keep
        return r * twice(scale)

    def update(g, r, v):
        first = 8 * g
        inside = jnp.logical_and(lane >= first, lane < first + 8)
        terms = [twice(spread(v, first + t)) * r[t : t + 1] for t in range(8)]
        while len(terms) > 1:
            terms = [terms[i] + terms[i + 1] for i in range(0, len(terms), 2)]
        return jnp.where(inside, 0.0, v) - terms[0]

    r = pivots(0, a_ref[0:8, :])
    for g in range(groups - 1):
        nxt = slice(8 * g + 8, 8 * g + 16)
        ahead = pivots(g + 1, update(g, r, a_ref[nxt, :]))
        for h in range(g + 2, groups):
            rows = slice(8 * h, 8 * h + 8)
            a_ref[rows, :] = update(g, r, a_ref[rows, :])
        r = ahead


def rotate_kernel(total_slots, gram, filt, out, work):
    states = filt.shape[0]
    work[...] = gram[...] * (1.0 / total_slots)
    work[0:128, 128:states] = work[128:states, 0:128].T
    full = work[...]
    row = lax.broadcasted_iota(i32, full.shape, 0)
    col = lax.broadcasted_iota(i32, full.shape, 1)
    diag = jnp.where(row == col, full, 0.0)
    across = jnp.sum(diag, axis=0, keepdims=True)
    across = lax.rsqrt(jnp.where(col[0:1] < states, across, 1.0))
    down = lax.rsqrt(jnp.sum(diag, axis=1, keepdims=True))
    work[...] = full * across * down
    eliminate(work, states)
    done = work[...]
    pivot = jnp.sum(jnp.where(row == col, done, 0.0), axis=1, keepdims=True)
    lower = jnp.where(col < row, done, jnp.where(col == row, 1.0, 0.0))
    inverse = (lower * lax.rsqrt(pivot) * across)[:, :states].astype(bf16)
    out[...] = matmul(inverse, filt[...]).astype(bf16)


def rotated(total_slots, gram, filt):
    whole = pl.BlockSpec(memory_space=pltpu.VMEM)
    return pl.pallas_call(
        functools.partial(rotate_kernel, total_slots),
        out_shape=jax.ShapeDtypeStruct(filt.shape, bf16),
        in_specs=[whole] * 2,
        out_specs=whole,
        scratch_shapes=[pltpu.VMEM(gram.shape, f32)],
        name="rotate",
    )(gram, filt)


def on_device(sizes, states, cell_matrices, connectivity, side_nodes, top_nodes, pot_index, pot_table):
    filt, gram = filtered_gram(
        sizes, pot_table, connectivity, side_nodes, top_nodes, pot_index[None, :], states, cell_matrices
    )
    total_slots = states.shape[1] * sizes[0] * sizes[1] * sizes[2]
    return rotated(total_slots, gram, filt)


def solution(mesh):
    sizes = tuple(mesh.shape[name] for name in ("gx", "gy", "gz"))
    in_specs = (
        P(None, ("gx", "gy", "gz")),
        P(("gx", "gy", "gz"), None, None),
        P(("gx", "gy", "gz"), None),
        P(None, ("gx", "gy", "gz")),
        P(None, ("gx", "gy", "gz")),
        P(("gx", "gy", "gz")),
        P(),
    )
    out_specs = P(None, ("gx", "gy", "gz"))
    return jax.shard_map(
        functools.partial(on_device, sizes), mesh=mesh, in_specs=in_specs, out_specs=out_specs, check_vma=False
    )
```
